32 devices in a mesh: frame: 16 (over z, x, core), head: 2 (over y).
Axes of the slice: x: 2, y: 2, z: 4, core: 2. Of those that a mesh axis runs over, the one named last changes fastest.
Arguments:
- activations: bfloat16 [32, 128, 4096], P('frame'), may hold values from -6 to 6
- w_query: bfloat16 [4096, 4096], P('frame', 'head'), may hold values from -0.09375 to 0.09375
- w_key: bfloat16 [4096, 4096], P('frame', 'head'), may hold values from -0.09375 to 0.09375
- w_value: bfloat16 [4096, 4096], P('frame', 'head'), may hold values from -0.09375 to 0.09375
- q_gain: float32 [128], replicated, may hold values from 0.1 to 1.9
- k_gain: float32 [128], replicated, may hold values from 0.1 to 1.9
- grad_attn: bfloat16 [32, 128, 4096], P('frame', None, 'head'), may hold values from -6 to 6
Outputs:
- grad_input: bfloat16 [32, 128, 4096], P('frame', None, 'head')
- grad_wq: float32 [4096, 4096], P('frame', 'head')
- grad_wk: float32 [4096, 4096], P('frame', 'head')
- grad_wv: float32 [4096, 4096], P('frame', 'head')
The draws below stay inside these ranges and needn't reach their ends.
All inputs are finite; a program needn't handle non-finite values.
Results may differ from the reference program's by a relative error of at most 0.018.
Values may be sent and summed in bfloat16 or wider, within the bound.
A program may use at most 192 MiB of HBM per device.

```python
import math
import jax
import jax.numpy as jnp
from jax import lax

D = 4096
HEADS = 32
HD = 128
FR_DEV = 2
PATCHES = 128
FRAMES = 32
N_FRAME = 16


def shard_levels(own_key, extent, shards, least, top_value):
    level = 1.0
    for axis_at, shards_of in shards:
        heights = jax.random.uniform(jax.random.fold_in(jax.random.fold_in(own_key, 6), axis_at), (shards_of,), jnp.float32, least / len(shards), top_value / len(shards))
        level = level * jnp.repeat(jnp.exp(heights), extent[axis_at] // shards_of).reshape((-1,) + (1,) * (len(extent) - 1 - axis_at))
    return level


def scatter_about(stream_key, dims, spread, limit, pieces=(), kind=jnp.bfloat16):
    level = shard_levels(stream_key, dims, pieces, -0.22, 0.18) if pieces else 1.0
    result = jax.random.normal(stream_key, dims, jnp.float32) * spread * level
    return jnp.minimum(jnp.maximum(result, -limit), limit).astype(kind)


def setup_inputs(seed: int = 0) -> dict:
    key_list = jax.random.split(jax.random.key(seed), 8)
    return {
        "activations": scatter_about(key_list[0], (FRAMES, PATCHES, D), 1.0, 6.0, ((0, 16),)),
        "w_query": scatter_about(key_list[1], (D, D), D ** -0.5, 0.09375, ((0, 16), (1, 2))),
        "w_key": scatter_about(key_list[2], (D, D), D ** -0.5, 0.09375, ((0, 16), (1, 2))),
        "w_value": scatter_about(key_list[3], (D, D), D ** -0.5, 0.09375, ((0, 16), (1, 2))),
        "q_gain": jnp.clip(1.0 + 0.18 * jax.random.normal(key_list[4], (HD,), jnp.float32), 0.1, 1.9),
        "k_gain": jnp.clip(1.0 + 0.18 * jax.random.normal(key_list[5], (HD,), jnp.float32), 0.1, 1.9),
        "grad_attn": scatter_about(key_list[6], (FRAMES, PATCHES, D), 1.0, 6.0, ((0, 16), (2, 2))),
    }


epsilon = 1e-06

def scaled(raw, gain):
    inverse = lax.rsqrt(lax.optimization_barrier(jnp.mean(raw * raw, axis=-1, keepdims=True)) + epsilon)
    return raw * inverse * gain

def attend(query, key_norm, value):
    factor = 1.0 / math.sqrt(query.shape[-1])
    scores = jnp.einsum('fphd,gphd->phfg', query, key_norm) * factor
    expon = jnp.exp(scores)
    weights = expon / lax.optimization_barrier(jnp.sum(expon, axis=-1, keepdims=True))
    return jnp.einsum('phfg,gphd->fphd', weights, value)

def attend_back(query, key_norm, value, cotan):
    _, pull = jax.vjp(attend, query.astype(jnp.float32), key_norm.astype(jnp.float32), value.astype(jnp.float32))
    grads = pull(cotan.astype(jnp.float32))
    return (grads[0].astype(jnp.bfloat16), grads[1].astype(jnp.bfloat16), grads[2].astype(jnp.bfloat16))

def reference(activations, w_query, w_key, w_value, q_gain, k_gain, grad_attn):
    head_dim = D // HEADS
    shape4 = (FRAMES, PATCHES, HEADS, head_dim)
    tok_rows = activations.reshape(FRAMES * PATCHES, D)
    q_raw = jnp.dot(tok_rows, w_query, preferred_element_type=jnp.float32).reshape(shape4)
    k_raw = jnp.dot(tok_rows, w_key, preferred_element_type=jnp.float32).reshape(shape4)
    q_norm = scaled(q_raw, q_gain).astype(jnp.bfloat16)
    k_norm = scaled(k_raw, k_gain).astype(jnp.bfloat16)
    value = jnp.dot(tok_rows, w_value, preferred_element_type=jnp.float32).astype(jnp.bfloat16).reshape(shape4)
    cotan = grad_attn.reshape(shape4)
    d_qn, d_kn, d_val = attend_back(q_norm, k_norm, value, cotan)
    _, pull_query = jax.vjp(lambda raw: scaled(raw, q_gain), q_raw)
    _, pull_key = jax.vjp(lambda raw: scaled(raw, k_gain), k_raw)
    d_q_raw = pull_query(d_qn.astype(jnp.float32))[0].astype(jnp.bfloat16).reshape(FRAMES * PATCHES, D)
    d_k_raw = pull_key(d_kn.astype(jnp.float32))[0].astype(jnp.bfloat16).reshape(FRAMES * PATCHES, D)
    d_v_rows = d_val.reshape(FRAMES * PATCHES, D)
    contract = (((1,), (1,)), ((), ()))
    grad_sum = lax.dot_general(d_q_raw, w_query, contract, preferred_element_type=jnp.float32)
    grad_sum = grad_sum + lax.dot_general(d_k_raw, w_key, contract, preferred_element_type=jnp.float32)
    grad_sum = grad_sum + lax.dot_general(d_v_rows, w_value, contract, preferred_element_type=jnp.float32)
    grad_input = grad_sum.astype(jnp.bfloat16).reshape(FRAMES, PATCHES, D)
    d_all = jnp.concatenate([d_q_raw, d_k_raw, d_v_rows], axis=1)
    groups = tok_rows.reshape(N_FRAME, FR_DEV * PATCHES, D)
    d_groups = d_all.reshape(N_FRAME, FR_DEV * PATCHES, 3 * D)

    def add_group(total, pair):
        term = lax.dot_general(pair[0], pair[1], (((0,), (0,)), ((), ())), preferred_element_type=jnp.float32)
        rounded = lax.optimization_barrier(term.astype(jnp.bfloat16)).astype(jnp.float32)
        return (total + rounded, None)
    total, _ = lax.scan(add_group, jnp.zeros((D, 3 * D), jnp.float32), (groups, d_groups))
    return (grad_input, total[:, :D], total[:, D:2 * D], total[:, 2 * D:])
```

```python
import math

import jax
import jax.numpy as jnp
from jax import lax
from jax.sharding import Mesh, PartitionSpec as P

HD = 128


epsilon = 1e-06


def scaled(raw, gain):
    inverse = lax.rsqrt(jnp.mean(raw * raw, axis=-1, keepdims=True) + epsilon)
    return raw * inverse * gain


def attend(query, key_norm, value):
    factor = 1.0 / math.sqrt(query.shape[-1])
    scores = jnp.einsum("fphd,gphd->phfg", query, key_norm) * factor
    expon = jnp.exp(scores)
    weights = expon / jnp.sum(expon, axis=-1, keepdims=True)
    return jnp.einsum("phfg,gphd->fphd", weights, value)


def attend_back(query, key_norm, value, cotan):
    _, pull = jax.vjp(
        attend, query.astype(jnp.float32), key_norm.astype(jnp.float32), value.astype(jnp.float32)
    )
    grads = pull(cotan.astype(jnp.float32))
    return (
        grads[0].astype(jnp.bfloat16),
        grads[1].astype(jnp.bfloat16),
        grads[2].astype(jnp.bfloat16),
    )


def line_split(n_frame, heads_here):
    part = 1
    while (
        4 * part * part <= n_frame
        and n_frame % (2 * part) == 0
        and heads_here % (2 * part) == 0
    ):
        part *= 2
    return part


def make_body(n_a, n_b):
    def body(activations, w_query, w_key, w_value, q_gain, k_gain, grad_attn):
        frames_here, patches, width = activations.shape
        rows_here, head_cols = w_query.shape
        cols = head_cols // n_a
        heads = cols // HD
        frames = frames_here * n_a
        tokens = frames * patches

        def stacked(x):
            return jnp.concatenate([x[:, i * cols : (i + 1) * cols] for i in range(n_a)], axis=0)

        def exchange(x):
            return lax.all_to_all(x, "fa", split_axis=0, concat_axis=0, tiled=True)

        acts = lax.all_gather(activations.reshape(-1, width), "fa", axis=0, tiled=True)
        cotan = exchange(stacked(grad_attn.reshape(-1, head_cols)))
        acts, cotan, *mine = lax.optimization_barrier(
            (acts, cotan, exchange(stacked(w_query)), stacked(w_key), stacked(w_value))
        )
        mine[1:] = [exchange(m) for m in mine[1:]]
        wq, wk, wv = (lax.all_gather(m, "fb", axis=0, tiled=True) for m in mine)

        def blocks(x, order):
            return jnp.concatenate(
                [x[:, i * rows_here : (i + 1) * rows_here] for i in order], axis=1
            )

        rows = blocks(acts, [i * n_b + j for j in range(n_b) for i in range(n_a)])

        def spread(x):
            return lax.all_to_all(x, "fb", split_axis=1, concat_axis=0, tiled=True)

        def back(x):
            return lax.all_to_all(x, "fb", split_axis=0, concat_axis=1, tiled=True)

        shape4 = (frames, patches, heads, HD)
        cotan = spread(cotan.reshape(shape4))

        q_raw = jnp.dot(rows, wq, preferred_element_type=jnp.float32).reshape(tokens, heads, HD)
        q_norm = spread(scaled(q_raw, q_gain).astype(jnp.bfloat16).reshape(shape4))
        k_raw = jnp.dot(rows, wk, preferred_element_type=jnp.float32).reshape(tokens, heads, HD)
        k_norm = spread(scaled(k_raw, k_gain).astype(jnp.bfloat16).reshape(shape4))
        value = jnp.dot(rows, wv, preferred_element_type=jnp.float32)
        value = spread(value.astype(jnp.bfloat16).reshape(shape4))

        grads = attend_back(q_norm, k_norm, value, cotan)
        d_val, d_qn, d_kn = back(grads[2]), back(grads[0]), back(grads[1])

        _, pull_query = jax.vjp(lambda raw: scaled(raw, q_gain), q_raw)
        _, pull_key = jax.vjp(lambda raw: scaled(raw, k_gain), k_raw)
        d_q = pull_query(d_qn.reshape(tokens, heads, HD).astype(jnp.float32))[0]
        d_q = d_q.astype(jnp.bfloat16).reshape(tokens, cols)
        d_k = pull_key(d_kn.reshape(tokens, heads, HD).astype(jnp.float32))[0]
        d_k = d_k.astype(jnp.bfloat16).reshape(tokens, cols)
        d_v = d_val.reshape(tokens, cols)

        def weight_grad(d):
            term = lax.dot_general(
                rows, d, (((0,), (0,)), ((), ())), preferred_element_type=jnp.float32
            ).astype(jnp.bfloat16)
            return lax.psum_scatter(term, "fb", scatter_dimension=0, tiled=True)

        def regroup(summed):
            out = exchange(summed)
            out = [out[i * rows_here : (i + 1) * rows_here] for i in range(n_a)]
            return jnp.concatenate(out, axis=1).astype(jnp.float32)

        sum_v, sum_q, sum_k = weight_grad(d_v), weight_grad(d_q), weight_grad(d_k)

        contract = (((1,), (1,)), ((), ()))
        partial = lax.dot_general(d_q, wq, contract, preferred_element_type=jnp.float32)
        partial = partial + lax.dot_general(d_k, wk, contract, preferred_element_type=jnp.float32)
        partial = partial + lax.dot_general(d_v, wv, contract, preferred_element_type=jnp.float32)
        partial = blocks(
            partial.astype(jnp.bfloat16), [j * n_a + i for i in range(n_a) for j in range(n_b)]
        )
        partial, sum_q, sum_k, sum_v = lax.optimization_barrier((partial, sum_q, sum_k, sum_v))
        partial = lax.psum_scatter(partial, "head", scatter_dimension=1, tiled=True)
        sums = (regroup(sum_q), regroup(sum_k), regroup(sum_v))
        partial, sums = lax.optimization_barrier((partial, sums))
        grad_input = lax.psum_scatter(partial, "fa", scatter_dimension=0, tiled=True)
        grad_input = grad_input.reshape(frames_here, patches, -1)
        return (grad_input, *sums)

    return body


def make_patch_body(n_frame):
    swap = [(0, 1), (1, 0)]

    def body(activations, w_query, w_key, w_value, q_gain, k_gain, grad_attn):
        frames_here, patches, width = activations.shape
        rows_here, head_cols = w_query.shape
        half = patches // 2
        cols = head_cols // n_frame
        frames = frames_here * n_frame
        tokens = frames * half
        side = lax.axis_index("head")

        def halves(x, axis, size):
            mine = lax.dynamic_slice_in_dim(x, side * size, size, axis)
            other = lax.dynamic_slice_in_dim(x, (1 - side) * size, size, axis)
            return mine, other

        def rejoin(mine, other, axis):
            return jnp.where(
                side == 0,
                jnp.concatenate([mine, other], axis),
                jnp.concatenate([other, mine], axis),
            )

        def exchange(x):
            return lax.all_to_all(x, "frame", split_axis=0, concat_axis=0, tiled=True)

        def across(x):
            return lax.ppermute(x, "head", swap)

        def by_head(x):
            return jnp.concatenate([x[:, i * cols : (i + 1) * cols] for i in range(n_frame)], axis=0)

        own_acts, _ = halves(activations, 1, half)
        acts = lax.all_gather(own_acts.reshape(-1, width), "frame", axis=0, tiled=True)

        cot_mine, cot_other = halves(grad_attn, 1, half)
        cot_other = across(cot_other)
        mine = [exchange(by_head(w)) for w in (w_query, w_key, w_value)]
        wq, wk, wv = (jnp.concatenate([w, across(w)], axis=1) for w in mine)
        cotan = jnp.concatenate(
            [
                exchange(by_head(x.reshape(-1, head_cols)))
                for x in (cot_mine, cot_other)
            ],
            axis=1,
        )

        heads = 2 * cols // HD
        shape4 = (frames, half, heads, HD)
        shape3 = (tokens, heads, HD)
        q_raw = jnp.dot(acts, wq, preferred_element_type=jnp.float32).reshape(shape3)
        k_raw = jnp.dot(acts, wk, preferred_element_type=jnp.float32).reshape(shape3)
        value = jnp.dot(acts, wv, preferred_element_type=jnp.float32)
        value = value.astype(jnp.bfloat16).reshape(shape4)
        q_norm = scaled(q_raw, q_gain).astype(jnp.bfloat16).reshape(shape4)
        k_norm = scaled(k_raw, k_gain).astype(jnp.bfloat16).reshape(shape4)
        d_qn, d_kn, d_val = attend_back(q_norm, k_norm, value, cotan.reshape(shape4))

        _, pull_query = jax.vjp(lambda raw: scaled(raw, q_gain), q_raw)
        _, pull_key = jax.vjp(lambda raw: scaled(raw, k_gain), k_raw)
        d_q = pull_query(d_qn.reshape(shape3).astype(jnp.float32))[0]
        d_q = d_q.astype(jnp.bfloat16).reshape(tokens, 2 * cols)
        d_k = pull_key(d_kn.reshape(shape3).astype(jnp.float32))[0]
        d_k = d_k.astype(jnp.bfloat16).reshape(tokens, 2 * cols)
        d_v = d_val.reshape(tokens, 2 * cols)

        d_all = jnp.concatenate([d_q, d_k, d_v], axis=1)
        w_all = jnp.concatenate([wq, wk, wv], axis=1)
        partial = lax.dot_general(
            d_all, w_all, (((1,), (1,)), ((), ())), preferred_element_type=jnp.float32
        ).astype(jnp.bfloat16)
        partial = lax.psum_scatter(partial, "frame", scatter_dimension=0, tiled=True)
        mine_cols, other_cols = halves(partial, 1, head_cols)
        shape_out = (frames_here, half, head_cols)
        grad_input = rejoin(
            mine_cols.reshape(shape_out), across(other_cols).reshape(shape_out), 1
        )

        def weight_grad(d):
            term = lax.dot_general(
                acts, d, (((0,), (0,)), ((), ())), preferred_element_type=jnp.float32
            )
            total = term[:, :cols] + across(term[:, cols:].astype(jnp.bfloat16)).astype(jnp.float32)
            out = exchange(total.astype(jnp.bfloat16))
            out = [out[i * rows_here : (i + 1) * rows_here] for i in range(n_frame)]
            return jnp.concatenate(out, axis=1).astype(jnp.float32)

        return (grad_input, weight_grad(d_q), weight_grad(d_k), weight_grad(d_v))

    return body


def solution(mesh):
    n_frame, n_head = mesh.shape["frame"], mesh.shape["head"]

    def by_patch(activations, w_query, w_key, w_value, q_gain, k_gain, grad_attn):
        placed = (
            P("frame", None, None),
            P("frame", "head"),
            P("frame", "head"),
            P("frame", "head"),
            P(),
            P(),
            P("frame", None, "head"),
        )
        return jax.shard_map(
            make_patch_body(n_frame),
            mesh=mesh,
            in_specs=placed,
            out_specs=(placed[6], placed[1], placed[1], placed[1]),
            check_vma=False,
        )(activations, w_query, w_key, w_value, q_gain, k_gain, grad_attn)

    def run(activations, w_query, w_key, w_value, q_gain, k_gain, grad_attn):
        heads_here = w_query.shape[1] // (HD * n_head)
        if n_head == 2 and heads_here % n_frame == 0 and activations.shape[1] % n_head == 0:
            return by_patch(activations, w_query, w_key, w_value, q_gain, k_gain, grad_attn)
        n_a = line_split(n_frame, w_query.shape[1] // (HD * n_head))
        n_b = n_frame // n_a
        split = Mesh(mesh.devices.reshape(n_a, n_b, n_head), ("fa", "fb", "head"))
        frame = ("fa", "fb")
        placed = (
            P(frame, None, None),
            P(frame, "head"),
            P(frame, "head"),
            P(frame, "head"),
            P(),
            P(),
            P(frame, None, "head"),
        )
        return jax.shard_map(
            make_body(n_a, n_b),
            mesh=split,
            in_specs=placed,
            out_specs=(
                P(frame, None, "head"),
                P(frame, "head"),
                P(frame, "head"),
                P(frame, "head"),
            ),
            check_vma=False,
        )(activations, w_query, w_key, w_value, q_gain, k_gain, grad_attn)

    return run
```

```python
import functools
import math

import jax
import jax.numpy as jnp
from jax import lax
from jax.experimental import pallas as pl
from jax.experimental.pallas import tpu as pltpu
from jax.sharding import Mesh, PartitionSpec as P

MESH = pl.DeviceIdType.MESH
ANY = pl.BlockSpec(memory_space=pl.ANY)

HD = 128


epsilon = 1e-06


def scaled(raw, gain):
    inverse = lax.rsqrt(jnp.mean(raw * raw, axis=-1, keepdims=True) + epsilon)
    return raw * inverse * gain


def attend(query, key_norm, value):
    factor = 1.0 / math.sqrt(query.shape[-1])
    scores = jnp.einsum("fphd,gphd->phfg", query, key_norm) * factor
    expon = jnp.exp(scores)
    weights = expon / jnp.sum(expon, axis=-1, keepdims=True)
    return jnp.einsum("phfg,gphd->fphd", weights, value)


def attend_back(query, key_norm, value, cotan):
    _, pull = jax.vjp(
        attend, query.astype(jnp.float32), key_norm.astype(jnp.float32), value.astype(jnp.float32)
    )
    grads = pull(cotan.astype(jnp.float32))
    return (
        grads[0].astype(jnp.bfloat16),
        grads[1].astype(jnp.bfloat16),
        grads[2].astype(jnp.bfloat16),
    )


def line_split(n_frame, heads_here):
    part = 1
    while (
        4 * part * part <= n_frame
        and n_frame % (2 * part) == 0
        and heads_here % (2 * part) == 0
    ):
        part *= 2
    return part


def make_body(n_a, n_b):
    def body(activations, w_query, w_key, w_value, q_gain, k_gain, grad_attn):
        frames_here, patches, width = activations.shape
        rows_here, head_cols = w_query.shape
        cols = head_cols // n_a
        heads = cols // HD
        frames = frames_here * n_a
        tokens = frames * patches

        def stacked(x):
            return jnp.concatenate([x[:, i * cols : (i + 1) * cols] for i in range(n_a)], axis=0)

        def exchange(x):
            return lax.all_to_all(x, "fa", split_axis=0, concat_axis=0, tiled=True)

        acts = lax.all_gather(activations.reshape(-1, width), "fa", axis=0, tiled=True)
        cotan = exchange(stacked(grad_attn.reshape(-1, head_cols)))
        acts, cotan, *mine = lax.optimization_barrier(
            (acts, cotan, exchange(stacked(w_query)), stacked(w_key), stacked(w_value))
        )
        mine[1:] = [exchange(m) for m in mine[1:]]
        wq, wk, wv = (lax.all_gather(m, "fb", axis=0, tiled=True) for m in mine)

        def blocks(x, order):
            return jnp.concatenate(
                [x[:, i * rows_here : (i + 1) * rows_here] for i in order], axis=1
            )

        rows = blocks(acts, [i * n_b + j for j in range(n_b) for i in range(n_a)])

        def spread(x):
            return lax.all_to_all(x, "fb", split_axis=1, concat_axis=0, tiled=True)

        def back(x):
            return lax.all_to_all(x, "fb", split_axis=0, concat_axis=1, tiled=True)

        shape4 = (frames, patches, heads, HD)
        cotan = spread(cotan.reshape(shape4))

        q_raw = jnp.dot(rows, wq, preferred_element_type=jnp.float32).reshape(tokens, heads, HD)
        q_norm = spread(scaled(q_raw, q_gain).astype(jnp.bfloat16).reshape(shape4))
        k_raw = jnp.dot(rows, wk, preferred_element_type=jnp.float32).reshape(tokens, heads, HD)
        k_norm = spread(scaled(k_raw, k_gain).astype(jnp.bfloat16).reshape(shape4))
        value = jnp.dot(rows, wv, preferred_element_type=jnp.float32)
        value = spread(value.astype(jnp.bfloat16).reshape(shape4))

        grads = attend_back(q_norm, k_norm, value, cotan)
        d_val, d_qn, d_kn = back(grads[2]), back(grads[0]), back(grads[1])

        _, pull_query = jax.vjp(lambda raw: scaled(raw, q_gain), q_raw)
        _, pull_key = jax.vjp(lambda raw: scaled(raw, k_gain), k_raw)
        d_q = pull_query(d_qn.reshape(tokens, heads, HD).astype(jnp.float32))[0]
        d_q = d_q.astype(jnp.bfloat16).reshape(tokens, cols)
        d_k = pull_key(d_kn.reshape(tokens, heads, HD).astype(jnp.float32))[0]
        d_k = d_k.astype(jnp.bfloat16).reshape(tokens, cols)
        d_v = d_val.reshape(tokens, cols)

        def weight_grad(d):
            term = lax.dot_general(
                rows, d, (((0,), (0,)), ((), ())), preferred_element_type=jnp.float32
            ).astype(jnp.bfloat16)
            return lax.psum_scatter(term, "fb", scatter_dimension=0, tiled=True)

        def regroup(summed):
            out = exchange(summed)
            out = [out[i * rows_here : (i + 1) * rows_here] for i in range(n_a)]
            return jnp.concatenate(out, axis=1).astype(jnp.float32)

        sum_v, sum_q, sum_k = weight_grad(d_v), weight_grad(d_q), weight_grad(d_k)

        contract = (((1,), (1,)), ((), ()))
        partial = lax.dot_general(d_q, wq, contract, preferred_element_type=jnp.float32)
        partial = partial + lax.dot_general(d_k, wk, contract, preferred_element_type=jnp.float32)
        partial = partial + lax.dot_general(d_v, wv, contract, preferred_element_type=jnp.float32)
        partial = blocks(
            partial.astype(jnp.bfloat16), [j * n_a + i for i in range(n_a) for j in range(n_b)]
        )
        partial, sum_q, sum_k, sum_v = lax.optimization_barrier((partial, sum_q, sum_k, sum_v))
        partial = lax.psum_scatter(partial, "head", scatter_dimension=1, tiled=True)
        sums = (regroup(sum_q), regroup(sum_k), regroup(sum_v))
        partial, sums = lax.optimization_barrier((partial, sums))
        grad_input = lax.psum_scatter(partial, "fa", scatter_dimension=0, tiled=True)
        grad_input = grad_input.reshape(frames_here, patches, -1)
        return (grad_input, *sums)

    return body


def greet(peers):
    barrier = pltpu.get_barrier_semaphore()
    for peer in peers:
        pl.semaphore_signal(barrier, inc=1, device_id=peer, device_id_type=MESH)
    pl.semaphore_wait(barrier, len(peers))


def place(n_frame):
    me, side = lax.axis_index("frame"), lax.axis_index("head")
    z, x, c = me // 4, (me // 2) % 2, me % 2
    peers = [(lax.rem(me + j, n_frame), side) for j in range(1, n_frame)] + [(me, 1 - side)]
    return me, side, z, x, c, peers


def gather_kernel(n_frame, acts, cot, wq, wk, wv, acts_all, w_all, cot_all, cot_far, *sems):
    send_z, recv_z, send_x, recv_x, send_c, recv_c = sems[:6]
    send_w, recv_w, send_y, recv_y, send_t, recv_t, local = sems[6:]
    n_z = n_frame // 4
    me, side, z, x, c, peers = place(n_frame)
    rows = wq.shape[0]
    toks = acts.shape[0]
    weights = (wq, wk, wv)

    def index(zz, xx, cc):
        return (zz * 2 + xx) * 2 + cc

    def remote(src, dst, send, recv, to):
        return pltpu.make_async_remote_copy(
            src_ref=src, dst_ref=dst, send_sem=send, recv_sem=recv, device_id=to, device_id_type=MESH
        )

    def w_rows(f, part, width):
        return w_all.at[pl.ds(pl.multiple_of(f * rows, rows), rows), pl.ds(part, width)]

    def t_rows(f, part):
        return cot_all.at[pl.ds(pl.multiple_of(f * toks, toks), toks), pl.ds(part * HD, HD)]

    def w_from(src):
        f = pl.multiple_of(src * HD, HD)
        return [w.at[:, pl.ds(f, HD)] for w in weights]

    def a_from(zz, xx, cc, own=False):
        return acts if own else acts_all.at[index(zz, xx, cc)]

    greet(peers)
    partner = (me, 1 - side)
    far = remote(cot.at[1], cot_far, send_t.at[0], recv_t.at[0], partner)
    far.start()

    def hop(way, step):
        step_z = 2 * way - 1
        block = z - step_z * (step - 1)
        src = acts if step == 1 else acts_all.at[index(block, x, c)]
        valid = (z + 1 < n_z) if way else (z >= 1)
        if step > 1:
            valid = valid & ((block >= 0) if way else (block < n_z))
        at = way * (n_z - 1) + step - 1
        to = (index(z + step_z, x, c), side)
        return valid, lambda: remote(src, acts_all.at[index(block, x, c)], send_z.at[at], recv_z.at[at], to)

    def landed(way, step):
        step_z = 2 * way - 1
        block = z - step_z * step
        valid = (block >= 0) if way else (block < n_z)
        at = way * (n_z - 1) + step - 1
        return valid, block, lambda: remote(
            acts, acts_all.at[index(block, x, c)], send_z.at[at], recv_z.at[at], (me, 1 - side)
        )

    def beside(slot, block, own=False):
        return remote(
            a_from(block, x, c, own), acts_all.at[index(block, x, c)],
            send_x.at[slot], recv_x.at[slot], (index(z, 1 - x, c), side),
        )

    def over(slot, block, xx, own=False):
        return remote(
            a_from(block, xx, c, own), acts_all.at[index(block, xx, c)],
            send_c.at[slot], recv_c.at[slot], (index(z, x, 1 - c), side),
        )

    def slot_of(block):
        return lax.rem(block - z + n_z, n_z)

    def send_weights(j):
        to = lax.rem(me + j, n_frame)
        for i, src in enumerate(w_from(to)):
            remote(src, w_rows(me, i * HD, HD), send_w.at[j, i], recv_w.at[j, i], (to, side)).start()
        remote(cot.at[0, to], t_rows(me, 0), send_t.at[j], recv_t.at[j], (to, side)).start()

    for way in range(2):
        valid, make = hop(way, 1)
        pl.when(valid)(lambda make=make: make().start())
    beside(0, z, True).start()
    over(0, z, x, True).start()

    keep = [pltpu.make_async_copy(acts, acts_all.at[me], local.at[0])]
    for i, src in enumerate(w_from(me)):
        keep.append(pltpu.make_async_copy(src, w_rows(me, i * HD, HD), local.at[1 + i]))
    keep.append(pltpu.make_async_copy(cot.at[0, me], t_rows(me, 0), local.at[4]))
    for copy in keep:
        copy.start()

    third = (n_frame - 1 + 2) // 3
    order = []
    for j in range(1, n_frame // 2 + 1):
        order.append(j)
        if j != n_frame - j:
            order.append(n_frame - j)
    batches = [order[i * third : (i + 1) * third] for i in range(3)]
    for j in batches[0]:
        send_weights(j)
    for step in range(1, n_z):
        for way in range(2):
            valid, block, make = landed(way, step)

            def pass_on(way=way, step=step, block=block, make=make):
                make().wait_recv()
                if step + 1 < n_z:
                    more, again = hop(way, step + 1)
                    pl.when(more)(lambda: again().start())
                beside(slot_of(block), block).start()
                over(slot_of(block), block, x).start()

            pl.when(valid)(pass_on)
        for j in batches[step] if step < 3 else ():
            send_weights(j)
    for batch in batches[n_z:] if n_z < 3 else ():
        for j in batch:
            send_weights(j)

    far.wait_recv()
    for j in range(1, n_frame):
        to = lax.rem(me + j, n_frame)
        remote(
            cot_far.at[to], t_rows(me, 1), send_t.at[n_frame + j - 1], recv_t.at[n_frame + j - 1], (to, side)
        ).start()
    kept_far = pltpu.make_async_copy(cot_far.at[me], t_rows(me, 1), local.at[5])
    kept_far.start()

    for copy in keep:
        copy.wait()

    def share(j):
        f = lax.rem(me + n_frame - j, n_frame)
        return remote(
            w_rows(f, 0, 3 * HD), w_rows(f, 3 * HD, 3 * HD), send_y.at[j], recv_y.at[j], partner
        )

    share(0).start()
    for j in order:
        f = lax.rem(me + n_frame - j, n_frame)
        for i, src in enumerate(w_from(f)):
            remote(src, w_rows(f, i * HD, HD), send_w.at[j, i], recv_w.at[j, i], partner).wait_recv()
        share(j).start()

    for slot in range(n_z):
        block = lax.rem(z + slot, n_z)
        remote(
            acts, acts_all.at[index(block, 1 - x, c)], send_x.at[slot], recv_x.at[slot], partner
        ).wait_recv()
        over(n_z + slot, block, 1 - x).start()
    for slot in range(n_z):
        block = lax.rem(z + slot, n_z)
        for group, xx in ((0, x), (n_z, 1 - x)):
            remote(
                acts, acts_all.at[index(block, xx, 1 - c)],
                send_c.at[group + slot], recv_c.at[group + slot], partner,
            ).wait_recv()
    for j in range(n_frame):
        share(j).wait_recv()
        share(j).wait_send()
    for j in range(1, n_frame):
        f = lax.rem(me + n_frame - j, n_frame)
        for part, at in ((0, j), (1, n_frame + j - 1)):
            copy = remote(cot.at[0, f], t_rows(f, part), send_t.at[at], recv_t.at[at], partner)
            copy.wait_recv()
            copy.wait_send()
        for i, src in enumerate(w_from(f)):
            remote(src, w_rows(f, i * HD, HD), send_w.at[j, i], recv_w.at[j, i], partner).wait_send()
    far.wait_send()
    kept_far.wait()
    for way in range(2):
        for step in range(1, n_z):
            valid, make = hop(way, step)
            pl.when(valid)(lambda make=make: make().wait_send())
    for slot in range(n_z):
        block = lax.rem(z + slot, n_z)
        beside(slot, block, slot == 0).wait_send()
        over(slot, block, x, slot == 0).wait_send()
        over(n_z + slot, block, 1 - x).wait_send()


def gather_all(n_frame, acts, cot, wq, wk, wv):
    toks, width = acts.shape
    n_z = n_frame // 4
    dma = pltpu.SemaphoreType.DMA
    bf16 = jnp.bfloat16
    out = pl.pallas_call(
        functools.partial(gather_kernel, n_frame),
        out_shape=(
            jax.ShapeDtypeStruct((n_frame, toks, width), bf16),
            jax.ShapeDtypeStruct((width, 6 * HD), bf16),
            jax.ShapeDtypeStruct((n_frame * toks, 2 * HD), bf16),
            jax.ShapeDtypeStruct((n_frame, toks, HD), bf16),
        ),
        in_specs=[ANY] * 5,
        out_specs=(ANY,) * 4,
        scratch_shapes=[
            dma((2 * (n_z - 1),)), dma((2 * (n_z - 1),)),
            dma((n_z,)), dma((n_z,)),
            dma((2 * n_z,)), dma((2 * n_z,)),
            dma((n_frame, 3)), dma((n_frame, 3)),
            dma((n_frame,)), dma((n_frame,)),
            dma((2 * n_frame,)), dma((2 * n_frame,)),
            dma((6,)),
        ],
        compiler_params=pltpu.CompilerParams(collective_id=0, has_side_effects=True),
        name="gather_all",
    )(acts, cot, wq, wk, wv)
    return out[:3]


def attention_kernel(raw, cot, q_gain, k_gain, out):
    frames, some, _ = raw.shape
    n = frames * some

    def flat(x):
        return x.astype(jnp.float32).reshape(n, HD)

    def put(part, x):
        out[:, :, part * HD : (part + 1) * HD] = x.reshape(frames, some, HD).astype(out.dtype)

    def normed(x, gain):
        inverse = lax.rsqrt(jnp.mean(x * x, axis=-1, keepdims=True) + epsilon)
        return inverse, (x * inverse * gain).astype(jnp.bfloat16)

    def pulled(x, inverse, gain, d):
        d = d.astype(jnp.bfloat16).astype(jnp.float32) * gain
        along = jnp.sum(x * d, axis=-1, keepdims=True) * (1.0 / HD)
        return inverse * d - x * (inverse * inverse * inverse * along)

    def dot(a, b, ca, cb):
        return lax.dot_general(
            a, b, (((ca,), (cb,)), ((), ())), preferred_element_type=jnp.float32
        )

    q, k = flat(raw[:, :, :HD]), flat(raw[:, :, HD : 2 * HD])
    v = flat(raw[:, :, 2 * HD :]).astype(jnp.bfloat16)
    g = flat(cot[...]).astype(jnp.bfloat16)
    gq, gk = q_gain[...], k_gain[...]
    iq, qn = normed(q, gq)
    ik, kn = normed(k, gk)
    factor = 1.0 / math.sqrt(HD)
    row = lax.broadcasted_iota(jnp.int32, (n, n), 0)
    col = lax.broadcasted_iota(jnp.int32, (n, n), 1)
    same = lax.rem(row, some) == lax.rem(col, some)
    expon = jnp.where(same, jnp.exp(dot(qn, kn, 1, 1) * factor), 0.0)
    prob = expon / jnp.sum(expon, axis=-1, keepdims=True)
    d_prob = dot(g, v, 1, 1)
    mean = jnp.sum(prob * d_prob, axis=-1, keepdims=True)
    d_scores = (prob * (d_prob - mean) * factor).astype(jnp.bfloat16)
    put(2, dot(prob.astype(jnp.bfloat16), g, 0, 0))
    put(0, pulled(q, iq, gq, dot(d_scores, kn, 1, 0)))
    put(1, pulled(k, ik, gk, dot(d_scores, qn, 0, 0)))


def attention_back(raw, cot, q_gain, k_gain, frames):
    half = raw.shape[0] // frames
    heads = cot.shape[1] // HD
    some = 8
    return pl.pallas_call(
        attention_kernel,
        grid=(half // some, heads),
        out_shape=jax.ShapeDtypeStruct((frames, half, raw.shape[1]), jnp.bfloat16),
        in_specs=[
            pl.BlockSpec((frames, some, 3 * HD), lambda p, h: (0, p, h)),
            pl.BlockSpec((frames, some, HD), lambda p, h: (0, p, h)),
            pl.BlockSpec((1, HD), lambda p, h: (0, 0)),
            pl.BlockSpec((1, HD), lambda p, h: (0, 0)),
        ],
        out_specs=pl.BlockSpec((frames, some, 3 * HD), lambda p, h: (0, p, h)),
        compiler_params=pltpu.CompilerParams(dimension_semantics=("arbitrary", "arbitrary")),
        name="attention_back",
    )(
        raw.reshape(frames, half, -1),
        cot.reshape(frames, half, -1),
        q_gain.reshape(1, HD),
        k_gain.reshape(1, HD),
    ).reshape(frames * half, -1)


def make_patch_body(n_frame):
    swap = [(0, 1), (1, 0)]

    def body(activations, w_query, w_key, w_value, q_gain, k_gain, grad_attn):
        frames_here, patches, width = activations.shape
        rows_here, head_cols = w_query.shape
        half = patches // 2
        frames = frames_here * n_frame
        side = lax.axis_index("head")

        def halves(x, axis, size):
            mine = lax.dynamic_slice_in_dim(x, side * size, size, axis)
            other = lax.dynamic_slice_in_dim(x, (1 - side) * size, size, axis)
            return mine, other

        def rejoin(mine, other, axis):
            return jnp.where(
                side == 0,
                jnp.concatenate([mine, other], axis),
                jnp.concatenate([other, mine], axis),
            )

        def across(x):
            return lax.ppermute(x, "head", swap)

        def by_head(x):
            return x.reshape(-1, n_frame, HD).transpose(1, 0, 2)

        own_acts, _ = halves(activations, 1, half)
        cot = jnp.stack([by_head(x) for x in halves(grad_attn, 1, half)])
        acts, w_all, cotan = gather_all(
            n_frame, own_acts.reshape(-1, width), cot, w_query, w_key, w_value
        )
        acts = acts.reshape(-1, width)
        raw = jnp.dot(acts, w_all, preferred_element_type=jnp.float32)
        d_all = attention_back(raw, cotan, q_gain, k_gain, frames)

        partial = lax.dot_general(
            d_all, w_all, (((1,), (1,)), ((), ())), preferred_element_type=jnp.float32
        ).astype(jnp.bfloat16)
        terms = lax.dot_general(
            acts, d_all, (((0,), (0,)), ((), ())), preferred_element_type=jnp.float32
        ).astype(jnp.bfloat16)
        partial = lax.psum_scatter(partial, "frame", scatter_dimension=0, tiled=True)
        mine_cols, other_cols = halves(partial, 1, head_cols)
        shape_out = (frames_here, half, head_cols)
        grad_input = rejoin(
            mine_cols.reshape(shape_out), across(other_cols).reshape(shape_out), 1
        )
        cols = 3 * HD
        near = terms[:, :cols].astype(jnp.float32) + across(terms[:, cols:]).astype(jnp.float32)
        near = near.astype(jnp.bfloat16)
        near = lax.all_to_all(near, "frame", split_axis=0, concat_axis=0, tiled=True)
        near = near.reshape(n_frame, rows_here, 3, HD)
        grads = [
            near[:, :, i].transpose(1, 0, 2).reshape(rows_here, head_cols).astype(jnp.float32)
            for i in range(3)
        ]
        return (grad_input, *grads)

    return body


def solution(mesh):
    n_frame, n_head = mesh.shape["frame"], mesh.shape["head"]

    def by_patch(activations, w_query, w_key, w_value, q_gain, k_gain, grad_attn):
        placed = (
            P("frame", None, None),
            P("frame", "head"),
            P("frame", "head"),
            P("frame", "head"),
            P(),
            P(),
            P("frame", None, "head"),
        )
        return jax.shard_map(
            make_patch_body(n_frame),
            mesh=mesh,
            in_specs=placed,
            out_specs=(placed[6], placed[1], placed[1], placed[1]),
            check_vma=False,
        )(activations, w_query, w_key, w_value, q_gain, k_gain, grad_attn)

    def run(activations, w_query, w_key, w_value, q_gain, k_gain, grad_attn):
        heads_here = w_query.shape[1] // (HD * n_head)
        if (
            n_head == 2
            and heads_here == n_frame
            and n_frame % 4 == 0
            and activations.shape[1] % (8 * n_head) == 0
        ):
            return by_patch(activations, w_query, w_key, w_value, q_gain, k_gain, grad_attn)
        n_a = line_split(n_frame, w_query.shape[1] // (HD * n_head))
        n_b = n_frame // n_a
        split = Mesh(mesh.devices.reshape(n_a, n_b, n_head), ("fa", "fb", "head"))
        frame = ("fa", "fb")
        placed = (
            P(frame, None, None),
            P(frame, "head"),
            P(frame, "head"),
            P(frame, "head"),
            P(),
            P(),
            P(frame, None, "head"),
        )
        return jax.shard_map(
            make_body(n_a, n_b),
            mesh=split,
            in_specs=placed,
            out_specs=(
                P(frame, None, "head"),
                P(frame, "head"),
                P(frame, "head"),
                P(frame, "head"),
            ),
            check_vma=False,
        )(activations, w_query, w_key, w_value, q_gain, k_gain, grad_attn)

    return run
```
